32 devices in a mesh: ctx: 16 (over z, y, x), tp: 2 (over core).
Axes of the slice: x: 2, y: 2, z: 4, core: 2. Of those that a mesh axis runs over, the one named last changes fastest.
Arguments:
- tokens: bfloat16 [4096, 2688], P(('ctx', 'tp')), may hold values from -6 to 6
- result_grad: bfloat16 [4096, 2688], P(('ctx', 'tp')), may hold values from -6 to 6
- query_weight: bfloat16 [2688, 512], P(None, 'tp'), may hold values from -0.125 to 0.125
- key_weight: bfloat16 [2688, 256], P(None, 'tp'), may hold values from -0.125 to 0.125
- value_weight: bfloat16 [2688, 256], P(None, 'tp'), may hold values from -0.125 to 0.125
- output_weight: bfloat16 [512, 2688], P('tp'), may hold values from -0.5 to 0.5
- query_gain: float32 [128], replicated, may hold values from 0.5 to 1.5
- key_gain: float32 [128], replicated, may hold values from 0.5 to 1.5
Outputs:
- layer_output: bfloat16 [4096, 2688], P(('ctx', 'tp'))
- tokens_grad: bfloat16 [4096, 2688], P(('ctx', 'tp'))
The draws below stay inside these ranges and needn't reach their ends.
All inputs are finite; a program needn't handle non-finite values.
Results may differ from the reference program's by a relative error of at most 0.012.
Values may be sent and summed in bfloat16 or wider, within the bound.
A program may use at most 64 MiB of HBM per device.

```python
import jax
import jax.numpy as jnp
from jax import lax

D = 2688
HEAD = 128
WINDOW = 1024
T_DEV = 256
TOKENS = 4096
QHEADS = 4
KVHEADS = 2
N_TP = 2


def shard_levels(stream_key, extent, split, low, top_value):
    gain = 1.0
    for position, blocks in split:
        draws = jax.random.uniform(jax.random.fold_in(jax.random.fold_in(stream_key, 6), position), (blocks,), jnp.float32, low / len(split), top_value / len(split))
        gain = gain * jnp.repeat(jnp.exp(draws), extent[position] // blocks).reshape((-1,) + (1,) * (len(extent) - 1 - position))
    return gain


def noise(stream_key, shape, width, reach, cuts=(), held_as=jnp.bfloat16):
    gain = shard_levels(stream_key, shape, cuts, -0.22, 0.18) if cuts else 1.0
    array = jax.random.normal(stream_key, shape, jnp.float32) * width * gain
    return jnp.minimum(jnp.maximum(array, -reach), reach).astype(held_as)


def setup_inputs(seed: int = 0) -> dict:
    keys = jax.random.split(jax.random.key(seed), 9)
    return {
        "tokens": noise(keys[0], (TOKENS, D), 1.0, 6.0, ((0, 32),)),
        "result_grad": noise(keys[1], (TOKENS, D), 1.0, 6.0, ((0, 32),)),
        "query_weight": noise(keys[2], (D, QHEADS * HEAD), D ** -0.5, 0.125, ((1, 2),)),
        "key_weight": noise(keys[3], (D, KVHEADS * HEAD), D ** -0.5, 0.125, ((1, 2),)),
        "value_weight": noise(keys[4], (D, KVHEADS * HEAD), D ** -0.5, 0.125, ((1, 2),)),
        "output_weight": noise(keys[5], (QHEADS * HEAD, D), HEAD ** -0.5, 0.5, ((0, 2),)),
        "query_gain": jnp.clip(1.0 + 0.1 * jax.random.normal(keys[6], (HEAD,), jnp.float32), 0.5, 1.5),
        "key_gain": jnp.clip(1.0 + 0.1 * jax.random.normal(keys[7], (HEAD,), jnp.float32), 0.5, 1.5),
    }


norm_epsilon = 1e-06
score_scale = 168.0 ** (-0.5)
rope_theta = 10000.0

def rope_tables(positions, head_size):
    half_size = head_size // 2
    exponent = jnp.arange(half_size, dtype=jnp.float32) * (2.0 / head_size)
    frequency = jnp.power(jnp.float32(rope_theta), -exponent)
    angles = positions.astype(jnp.float32)[:, None] * frequency[None, :]
    return (jnp.cos(angles), jnp.sin(angles))

def norm_rope(raw_proj, scale_gain, cosines, sines):
    row_count = raw_proj.shape[0]
    head_size = scale_gain.shape[0]
    split_heads = raw_proj.reshape(row_count, -1, head_size)
    mean_square = lax.optimization_barrier(jnp.mean(split_heads * split_heads, axis=-1, keepdims=True))
    normed = split_heads * lax.rsqrt(mean_square + norm_epsilon) * scale_gain.astype(jnp.float32)
    half_size = head_size // 2
    low_half = normed[..., :half_size]
    high_half = normed[..., half_size:]
    cosine_b = cosines[:, None, :]
    sine_b = sines[:, None, :]
    return jnp.concatenate([low_half * cosine_b - high_half * sine_b, high_half * cosine_b + low_half * sine_b], axis=-1)

def attend(queries, keys_all, values_all, out_grad, query_first, key_first):
    query_count = queries.shape[0]
    key_count = keys_all.shape[0]
    queries_f = queries.astype(jnp.float32)
    keys_f = keys_all.astype(jnp.float32)
    values_f = values_all.astype(jnp.float32)
    out_grad_f = out_grad.astype(jnp.float32)
    scores = jnp.einsum('qkgh,ckh->kgqc', queries_f, keys_f) * score_scale
    query_pos = query_first + jnp.arange(query_count, dtype=jnp.int32)
    key_pos = key_first + jnp.arange(key_count, dtype=jnp.int32)
    distance = query_pos[:, None] - key_pos[None, :]
    allowed = (distance >= 0) & (distance < WINDOW) & (key_pos[None, :] >= 0)
    weights_raw = jnp.where(allowed, jnp.exp(scores), jnp.float32(0.0))
    denominator = lax.optimization_barrier(jnp.sum(weights_raw, axis=-1, keepdims=True))
    weights_soft = weights_raw / denominator
    weights_low = lax.optimization_barrier(weights_soft.astype(jnp.bfloat16))
    weights_low_f = weights_low.astype(jnp.float32)
    attended = lax.optimization_barrier(jnp.einsum('kgqc,ckh->qkgh', weights_low_f, values_f).astype(jnp.bfloat16))
    row_dots = lax.optimization_barrier(jnp.sum(out_grad_f * attended.astype(jnp.float32), axis=-1))
    prob_grad = jnp.einsum('qkgh,ckh->kgqc', out_grad_f, values_f)
    centered = prob_grad - jnp.transpose(row_dots, (1, 2, 0))[..., None]
    score_grad = lax.optimization_barrier((weights_soft * centered * score_scale).astype(jnp.bfloat16))
    score_grad_f = score_grad.astype(jnp.float32)
    query_grad = jnp.einsum('kgqc,ckh->qkgh', score_grad_f, keys_f)
    key_grad = jnp.einsum('kgqc,qkgh->ckh', score_grad_f, queries_f)
    value_grad = jnp.einsum('kgqc,qkgh->ckh', weights_low_f, out_grad_f)
    return (attended, query_grad, key_grad, value_grad)

def group_pass(tokens, result_grad, query_weight, key_weight, value_weight, output_weight, query_gain, key_gain):
    token_count = tokens.shape[0]
    kv_count = key_weight.shape[1] // HEAD
    per_kv = query_weight.shape[1] // key_weight.shape[1]
    positions = jnp.arange(token_count, dtype=jnp.int32)
    cosines, sines = rope_tables(positions, HEAD)
    query_raw = jnp.dot(tokens, query_weight, preferred_element_type=jnp.float32)
    key_raw = jnp.dot(tokens, key_weight, preferred_element_type=jnp.float32)
    value_raw = jnp.dot(tokens, value_weight, preferred_element_type=jnp.float32)
    queries = norm_rope(query_raw, query_gain, cosines, sines).astype(jnp.bfloat16).reshape(token_count, kv_count, per_kv, HEAD)
    keys_all = norm_rope(key_raw, key_gain, cosines, sines).astype(jnp.bfloat16)
    values_all = value_raw.astype(jnp.bfloat16).reshape(token_count, kv_count, HEAD)
    out_grad = jnp.dot(result_grad, output_weight.T, preferred_element_type=jnp.float32).astype(jnp.bfloat16)
    out_grad = out_grad.reshape(token_count, kv_count, per_kv, HEAD)
    padding = jnp.zeros((WINDOW, kv_count, HEAD), jnp.bfloat16)
    keys_pad = jnp.concatenate([padding, keys_all], axis=0)
    values_pad = jnp.concatenate([padding, values_all], axis=0)

    def one_block(running, block_index):
        key_acc, value_acc = running
        first_row = (block_index * T_DEV).astype(jnp.int32)
        query_block = lax.dynamic_slice_in_dim(queries, first_row, T_DEV, 0)
        grad_block = lax.dynamic_slice_in_dim(out_grad, first_row, T_DEV, 0)
        key_block = lax.dynamic_slice_in_dim(keys_pad, first_row, WINDOW + T_DEV, 0)
        value_block = lax.dynamic_slice_in_dim(values_pad, first_row, WINDOW + T_DEV, 0)
        attended, query_grad, key_grad, value_grad = attend(query_block, key_block, value_block, grad_block, first_row, first_row - WINDOW)
        key_acc = lax.dynamic_update_slice_in_dim(key_acc, lax.dynamic_slice_in_dim(key_acc, first_row, WINDOW + T_DEV, 0) + key_grad, first_row, 0)
        value_acc = lax.dynamic_update_slice_in_dim(value_acc, lax.dynamic_slice_in_dim(value_acc, first_row, WINDOW + T_DEV, 0) + value_grad, first_row, 0)
        return ((key_acc, value_acc), (attended, query_grad))
    zeros_acc = jnp.zeros((WINDOW + token_count, kv_count, HEAD), jnp.float32)
    block_ids = jnp.arange(token_count // T_DEV, dtype=jnp.int32)
    (key_acc, value_acc), (attended, query_grad) = lax.scan(one_block, (zeros_acc, zeros_acc), block_ids)
    attended_flat = attended.reshape(token_count, -1)
    query_grad = query_grad.reshape(token_count, -1, HEAD)

    def query_shape(raw_proj):
        return norm_rope(raw_proj, query_gain, cosines, sines)

    def key_shape(raw_proj):
        return norm_rope(raw_proj, key_gain, cosines, sines)
    query_back = jax.vjp(query_shape, query_raw)[1](query_grad)[0].astype(jnp.bfloat16)
    key_back = jax.vjp(key_shape, key_raw)[1](key_acc[WINDOW:])[0].astype(jnp.bfloat16)
    value_back = value_acc[WINDOW:].reshape(token_count, -1).astype(jnp.bfloat16)
    out_part = jnp.dot(attended_flat, output_weight, preferred_element_type=jnp.float32).astype(jnp.bfloat16)
    grad_part = jnp.dot(query_back, query_weight.T, preferred_element_type=jnp.float32)
    grad_part = grad_part + jnp.dot(key_back, key_weight.T, preferred_element_type=jnp.float32)
    grad_part = grad_part + jnp.dot(value_back, value_weight.T, preferred_element_type=jnp.float32)
    return (out_part, grad_part.astype(jnp.bfloat16))

def reference(tokens, result_grad, query_weight, key_weight, value_weight, output_weight, query_gain, key_gain):
    query_cols = query_weight.shape[1] // N_TP
    kv_cols = key_weight.shape[1] // N_TP
    out_sum = tokens.astype(jnp.float32)
    grad_sum = result_grad.astype(jnp.float32)
    for group_index in range(N_TP):
        query_part = query_weight[:, group_index * query_cols:(group_index + 1) * query_cols]
        key_part = key_weight[:, group_index * kv_cols:(group_index + 1) * kv_cols]
        value_part = value_weight[:, group_index * kv_cols:(group_index + 1) * kv_cols]
        output_part = output_weight[group_index * query_cols:(group_index + 1) * query_cols]
        out_part, grad_part = group_pass(tokens, result_grad, query_part, key_part, value_part, output_part, query_gain, key_gain)
        out_sum = out_sum + out_part.astype(jnp.float32)
        grad_sum = grad_sum + grad_part.astype(jnp.float32)
    return (out_sum.astype(jnp.bfloat16), grad_sum.astype(jnp.bfloat16))
```

```python
import functools

import jax
import jax.numpy as jnp
from jax import lax
from jax.experimental import pallas as pl
from jax.experimental.pallas import tpu as pltpu
from jax.sharding import PartitionSpec as P

WINDOW = 1024
norm_epsilon = 1e-06
score_scale = 168.0 ** (-0.5)
rope_theta = 10000.0
MESH = pl.DeviceIdType.MESH
f32 = jnp.float32
bf16 = jnp.bfloat16


def dot(a, b, ca, cb):
    return lax.dot_general(a, b, (((ca,), (cb,)), ((), ())), preferred_element_type=f32)


def rope(n, cosines, sines, half):
    return n * cosines + pltpu.roll(n, half, 1) * sines


def rope_back(g, cosines, sines, half):
    return g * cosines + pltpu.roll(g * sines, half, 1)


def inverse_rms(u):
    return lax.rsqrt(jnp.mean(u * u, axis=-1, keepdims=True) + norm_epsilon)


def norm_rope_back(g, u, gain, cosines, sines, half):
    r = inverse_rms(u)
    w = rope_back(g, cosines, sines, half) * gain
    return r * (w - u * (r * r * jnp.mean(w * u, axis=-1, keepdims=True)))


def kernel(
    n_ctx, n_tp, reach, per_kv, kv_count, head, tile,
    tokens, rgrad, qw, kw, vw, ow, qgain, kgain, freq,
    out_ref, gout_ref,
    wqkv, wo, xg, gg, raw, cos_t, sin_t, q_s, do_s, dot_s, kv_own, halo, e_s, dp_s,
    l_s, ot_s, dqt_s, att, dkv, sum4, own_grad, gin, rin, zbuf, back, part, rs_in, stage,
    local_sem, ag_send, ag_recv, f_send, f_relay, f_recv, b_send, g_recv, r_recv,
    rs_send, rs_recv, out_sem,
):
    c = lax.axis_index("ctx")
    t = lax.axis_index("tp")
    s = lax.rem(c, reach)
    z = lax.div(c, reach)
    nz = n_ctx // reach
    local, width = xg.shape[1], xg.shape[2]
    rows = local * n_tp
    half = head // 2
    qc = kv_count * per_kv * head
    kc = kv_count * head
    qn = per_kv * rows

    def local_copy(i, src, dst):
        return pltpu.make_async_copy(src, dst, local_sem.at[i])

    loads = [
        local_copy(0, tokens, xg.at[t]),
        local_copy(1, kw, wqkv.at[:, qc : qc + kc]),
        local_copy(2, vw, wqkv.at[:, qc + kc : qc + 2 * kc]),
        local_copy(3, qw, wqkv.at[:, :qc]),
        local_copy(4, rgrad, gg.at[t]),
        local_copy(5, ow, wo),
    ]
    for load in loads:
        load.start()

    def to_ctx(src, dst, send, recv, target):
        return pltpu.make_async_remote_copy(
            src_ref=src, dst_ref=dst, send_sem=send, recv_sem=recv,
            device_id={"ctx": target}, device_id_type=MESH,
        )

    def to_tp(src, dst, send, recv, target):
        return pltpu.make_async_remote_copy(
            src_ref=src, dst_ref=dst, send_sem=send, recv_sem=recv,
            device_id={"tp": target}, device_id_type=MESH,
        )

    barrier = pltpu.get_barrier_semaphore()
    for j in range(1, n_tp):
        pl.semaphore_signal(
            barrier, inc=1, device_id={"tp": lax.rem(t + j, n_tp)}, device_id_type=MESH
        )
    for j in range(1, reach):
        mate = z * reach + lax.rem(s + j, reach)
        pl.semaphore_signal(barrier, inc=1, device_id={"ctx": mate}, device_id_type=MESH)

    @pl.when(z + 1 < nz)
    def _():
        pl.semaphore_signal(barrier, inc=1, device_id={"ctx": c + reach}, device_id_type=MESH)

    @pl.when(z > 0)
    def _():
        pl.semaphore_signal(barrier, inc=1, device_id={"ctx": c - reach}, device_id_type=MESH)

    greeted = (
        n_tp - 1 + reach - 1
        + jnp.where(z > 0, jnp.int32(1), jnp.int32(0))
        + jnp.where(z + 1 < nz, jnp.int32(1), jnp.int32(0))
    )
    pl.semaphore_wait(barrier, greeted)

    gathers = []
    for w, (src, dst) in enumerate(((tokens, xg), (rgrad, gg))):
        for j in range(1, n_tp):
            copy = to_tp(src, dst.at[t], ag_send.at[w, j - 1], ag_recv.at[w, j - 1],
                         lax.rem(t + j, n_tp))
            copy.start()
            gathers.append((w, copy))

    position = (c * rows + lax.broadcasted_iota(jnp.int32, (rows, head), 0)).astype(f32)
    angles = position * freq[...]
    lane = lax.broadcasted_iota(jnp.int32, (rows, head), 1)
    cos_t[...] = jnp.cos(angles)
    sines = jnp.sin(angles)
    sin_t[...] = jnp.where(lane < half, -sines, sines)

    for i in (0, 1, 2):
        loads[i].wait()
    for w, copy in gathers:
        if w == 0:
            copy.wait_recv()
    x_all = xg[...].reshape(rows, width)
    raw[:, qc : qc + 2 * kc] = dot(x_all, wqkv[:, qc : qc + 2 * kc], 1, 0)
    for m in range(kv_count):
        u = raw[:, qc + m * head : qc + (m + 1) * head]
        n = u * inverse_rms(u) * kgain[...]
        kv_own[0, m] = rope(n, cos_t[...], sin_t[...], half).astype(bf16)
        v0 = qc + kc + m * head
        kv_own[1, m] = raw[:, v0 : v0 + head].astype(bf16)

    def ahead():
        return to_ctx(kv_own, halo.at[reach - 1], f_send.at[reach - 1], f_recv.at[reach - 1],
                      c + reach)

    def own_to(k):
        return to_ctx(kv_own, halo.at[k - 1], f_send.at[k - 1], f_recv.at[k - 1], c + k)

    def relay_to(k):
        return to_ctx(halo.at[reach - 1], halo.at[reach - k - 1], f_relay.at[k - 1],
                      f_recv.at[reach - k - 1], c - k)

    def halo_wait(d):
        to_ctx(kv_own, halo.at[d - 1], f_send.at[d - 1], f_recv.at[d - 1], c).wait_recv()

    @pl.when(z + 1 < nz)
    def _():
        ahead().start()

    for k in range(1, reach):
        @pl.when(s + k < reach)
        def _(k=k):
            own_to(k).start()

    loads[3].wait()
    raw[:, :qc] = dot(xg[...].reshape(rows, width), wqkv[:, :qc], 1, 0)
    for h in range(kv_count * per_kv):
        m, g = h // per_kv, h % per_kv
        u = raw[:, h * head : (h + 1) * head]
        n = u * inverse_rms(u) * qgain[...]
        q_s[m, g * rows : (g + 1) * rows] = rope(n, cos_t[...], sin_t[...], half).astype(bf16)
    loads[4].wait()
    loads[5].wait()
    for w, copy in gathers:
        if w == 1:
            copy.wait_recv()
    d_out = dot(gg[...].reshape(rows, width), wo[...], 1, 1).astype(bf16)
    for h in range(kv_count * per_kv):
        m, g = h // per_kv, h % per_kv
        piece = d_out[:, h * head : (h + 1) * head]
        do_s[m, g * rows : (g + 1) * rows] = piece
        dot_s[m, :, g * rows : (g + 1) * rows] = piece.astype(f32).T

    def kv(d, w, m):
        return kv_own[w, m] if d == 0 else halo[d - 1, w, m]

    def first_pass(d):
        for m in range(kv_count):
            key, value = kv(d, 0, m), kv(d, 1, m)
            e = jnp.exp(dot(key, q_s[m], 1, 1) * score_scale)
            if d == 0 or d == reach:
                key_row = lax.broadcasted_iota(jnp.int32, (rows, qn), 0)
                query_row = lax.broadcasted_iota(jnp.int32, (rows, qn), 1) % rows
                keep = query_row >= key_row if d == 0 else query_row < key_row
                e = jnp.where(keep, e, f32(0.0))
            total = jnp.sum(e, axis=0, keepdims=True)
            low = e.astype(bf16)
            e_s[d, m] = low
            mixed = dot(value, low, 0, 0)
            dp_s[d, m] = dot(value, do_s[m], 1, 1) * score_scale
            if d == 0:
                l_s[m] = total
                ot_s[m] = mixed
            else:
                l_s[m] += total
                ot_s[m] += mixed

    first_pass(0)

    @pl.when(z > 0)
    def _():
        halo_wait(reach)
        for k in range(1, reach):
            @pl.when(k <= s)
            def _(k=k):
                relay_to(k).start()
        first_pass(reach)

    for d in range(1, reach):
        @pl.when(c >= d)
        def _(d=d):
            halo_wait(d)
            first_pass(d)

    inv, delta = [], []
    for m in range(kv_count):
        inv.append(1.0 / l_s[m])
        o_t = (ot_s[m] * inv[m]).astype(bf16).astype(f32)
        delta.append(jnp.sum(o_t * dot_s[m], axis=0, keepdims=True) * score_scale)
        for g in range(per_kv):
            h = m * per_kv + g
            att[:, h * head : (h + 1) * head] = o_t[:, g * rows : (g + 1) * rows].T.astype(bf16)
        l_s[m] = inv[m]
        dqt_s[m] = jnp.zeros_like(dqt_s[m])

    def second_pass(d, m):
        p = e_s[d, m].astype(f32) * inv[m]
        ds = (p * (dp_s[d, m] - delta[m])).astype(bf16)
        dk = dot(ds, q_s[m], 1, 0)
        dv = dot(p.astype(bf16), do_s[m], 1, 0)
        dqt_s[m] += dot(kv(d, 0, m), ds, 0, 0)
        return dk, dv

    def grad_home(d):
        return to_ctx(dkv.at[d - 1], gin.at[d - 1], b_send.at[d - 1], g_recv.at[d - 1], c - d)

    def grad_mate(d):
        k = reach - d
        return to_ctx(dkv.at[d - 1], rin.at[k - 1], b_send.at[d - 1], r_recv.at[k - 1], c + k)

    def grad_back():
        return to_ctx(zbuf, gin.at[reach - 1], b_send.at[reach - 1], g_recv.at[reach - 1],
                      c - reach)

    for d in range(reach - 1, 0, -1):
        @pl.when(c >= d)
        def _(d=d):
            for m in range(kv_count):
                dk, dv = second_pass(d, m)
                dkv[d - 1, 0, m] = dk.astype(bf16)
                dkv[d - 1, 1, m] = dv.astype(bf16)

            @pl.when(d <= s)
            def _():
                grad_home(d).start()

            @pl.when(d > s)
            def _():
                grad_mate(d).start()

    @pl.when(z > 0)
    def _():
        for m in range(kv_count):
            dk, dv = second_pass(reach, m)
            sum4[0, m] = dk
            sum4[1, m] = dv

    for m in range(kv_count):
        dk, dv = second_pass(0, m)
        own_grad[0, m] = dk
        own_grad[1, m] = dv

    def rs_copy(w, j):
        target = lax.rem(t + j, n_tp)
        return to_tp(part.at[w, target], rs_in.at[w, j - 1], rs_send.at[w, j - 1],
                     rs_recv.at[w, j - 1], target)

    def project(w, lhs, index, by_row):
        block = lhs[pl.ds(pl.multiple_of(index * local, local), local), :]

        def step(i, carry):
            cols = pl.ds(pl.multiple_of(i * tile, 128), tile)
            if by_row:
                part[w, index, :, cols] = dot(block, wo[:, cols], 1, 0).astype(bf16)
            else:
                part[w, index, :, cols] = dot(block, wqkv[cols, :], 1, 1).astype(bf16)
            return carry

        lax.fori_loop(0, width // tile, step, 0)

    for j in range(1, n_tp):
        project(0, att, lax.rem(t + j, n_tp), True)
        rs_copy(0, j).start()

    @pl.when(z > 0)
    def _():
        for k in range(1, reach):
            @pl.when(k <= s)
            def _(k=k):
                to_ctx(zbuf, rin.at[k - 1], b_send.at[k - 1], r_recv.at[k - 1], c).wait_recv()
                sum4[...] += rin[k - 1].astype(f32)
        zbuf[...] = sum4[...].astype(bf16)
        grad_back().start()

    for m in range(kv_count):
        for g in range(per_kv):
            h = m * per_kv + g
            grad = dqt_s[m, :, g * rows : (g + 1) * rows].T
            u = raw[:, h * head : (h + 1) * head]
            back[:, h * head : (h + 1) * head] = norm_rope_back(
                grad, u, qgain[...], cos_t[...], sin_t[...], half
            ).astype(bf16)

    project(0, att, t, True)

    def finish(w, base, dst):
        total = part[w, t].astype(f32)
        for j in range(1, n_tp):
            rs_copy(w, j).wait_recv()
            total += rs_in[w, j - 1].astype(f32)
        stage[w] = (base[t].astype(f32) + total).astype(bf16)
        copy = pltpu.make_async_copy(stage.at[w], dst, out_sem.at[w])
        copy.start()
        return copy

    written = [finish(0, xg, out_ref)]

    def gin_add(d):
        to_ctx(zbuf, gin.at[d - 1], b_send.at[d - 1], g_recv.at[d - 1], c).wait_recv()
        own_grad[...] += gin[d - 1].astype(f32)

    for d in range(1, reach):
        @pl.when(s + d < reach)
        def _(d=d):
            gin_add(d)

    @pl.when(z + 1 < nz)
    def _():
        gin_add(reach)

    for m in range(kv_count):
        k0 = qc + m * head
        u = raw[:, k0 : k0 + head]
        back[:, k0 : k0 + head] = norm_rope_back(
            own_grad[0, m], u, kgain[...], cos_t[...], sin_t[...], half
        ).astype(bf16)
        back[:, k0 + kc : k0 + kc + head] = own_grad[1, m].astype(bf16)

    for j in range(1, n_tp):
        project(1, back, lax.rem(t + j, n_tp), False)
        rs_copy(1, j).start()
    project(1, back, t, False)
    written.append(finish(1, gg, gout_ref))

    for w, copy in gathers:
        copy.wait_send()

    @pl.when(z + 1 < nz)
    def _():
        ahead().wait_send()

    for k in range(1, reach):
        @pl.when(s + k < reach)
        def _(k=k):
            own_to(k).wait_send()

        @pl.when((z > 0) & (k <= s))
        def _(k=k):
            relay_to(k).wait_send()

        @pl.when(c >= k)
        def _(k=k):
            grad_home(k).wait_send()

    @pl.when(z > 0)
    def _():
        grad_back().wait_send()

    for w in range(2):
        for j in range(1, n_tp):
            rs_copy(w, j).wait_send()
    for copy in written:
        copy.wait()


def on_device(
    tokens, result_grad, query_weight, key_weight, value_weight, output_weight, query_gain, key_gain
):
    n_ctx = lax.axis_size("ctx")
    n_tp = lax.axis_size("tp")
    local, width = tokens.shape
    rows = local * n_tp
    head = query_gain.shape[0]
    kv_count = key_weight.shape[1] // head
    per_kv = query_weight.shape[1] // key_weight.shape[1]
    reach = WINDOW // rows
    qc = kv_count * per_kv * head
    kc = kv_count * head
    qn = per_kv * rows
    tile = max(k for k in range(128, 1025, 128) if width % k == 0)
    exponent = jnp.arange(head // 2, dtype=f32) * (2.0 / head)
    frequency = jnp.power(f32(rope_theta), -exponent)
    frequency = jnp.concatenate([frequency, frequency])[None, :]
    any_spec = pl.BlockSpec(memory_space=pl.ANY)
    vmem_spec = pl.BlockSpec(memory_space=pltpu.VMEM)
    block = (2, kv_count, rows, head)
    dma = pltpu.SemaphoreType.DMA
    out = jax.ShapeDtypeStruct((local, width), bf16)
    return pl.pallas_call(
        functools.partial(kernel, n_ctx, n_tp, reach, per_kv, kv_count, head, tile),
        out_shape=(out, out),
        in_specs=[any_spec] * 6 + [vmem_spec] * 3,
        out_specs=(any_spec, any_spec),
        scratch_shapes=[
            pltpu.VMEM((width, qc + 2 * kc), bf16),
            pltpu.VMEM((qc, width), bf16),
            pltpu.VMEM((n_tp, local, width), bf16),
            pltpu.VMEM((n_tp, local, width), bf16),
            pltpu.VMEM((rows, qc + 2 * kc), f32),
            pltpu.VMEM((rows, head), f32),
            pltpu.VMEM((rows, head), f32),
            pltpu.VMEM((kv_count, qn, head), bf16),
            pltpu.VMEM((kv_count, qn, head), bf16),
            pltpu.VMEM((kv_count, head, qn), f32),
            pltpu.VMEM(block, bf16),
            pltpu.VMEM((reach,) + block, bf16),
            pltpu.VMEM((reach + 1, kv_count, rows, qn), bf16),
            pltpu.VMEM((reach + 1, kv_count, rows, qn), f32),
            pltpu.VMEM((kv_count, 1, qn), f32),
            pltpu.VMEM((kv_count, head, qn), f32),
            pltpu.VMEM((kv_count, head, qn), f32),
            pltpu.VMEM((rows, qc), bf16),
            pltpu.VMEM((reach - 1,) + block, bf16),
            pltpu.VMEM(block, f32),
            pltpu.VMEM(block, f32),
            pltpu.VMEM((reach,) + block, bf16),
            pltpu.VMEM((reach - 1,) + block, bf16),
            pltpu.VMEM(block, bf16),
            pltpu.VMEM((rows, qc + 2 * kc), bf16),
            pltpu.VMEM((2, n_tp, local, width), bf16),
            pltpu.VMEM((2, n_tp - 1, local, width), bf16),
            pltpu.VMEM((2, local, width), bf16),
            dma((6,)),
            dma((2, n_tp - 1)),
            dma((2, n_tp - 1)),
            dma((reach,)),
            dma((reach - 1,)),
            dma((reach,)),
            dma((reach,)),
            dma((reach,)),
            dma((reach - 1,)),
            dma((2, n_tp - 1)),
            dma((2, n_tp - 1)),
            dma((2,)),
        ],
        compiler_params=pltpu.CompilerParams(
            collective_id=0, has_side_effects=True, vmem_limit_bytes=60 * 1024 * 1024
        ),
    )(
        tokens, result_grad, query_weight, key_weight, value_weight, output_weight,
        query_gain[None, :], key_gain[None, :], frequency,
    )


def solution(mesh):
    in_specs = (
        P(("ctx", "tp"), None),
        P(("ctx", "tp"), None),
        P(None, "tp"),
        P(None, "tp"),
        P(None, "tp"),
        P("tp", None),
        P(),
        P(),
    )
    out_specs = (P(("ctx", "tp"), None), P(("ctx", "tp"), None))
    return jax.shard_map(
        on_device, mesh=mesh, in_specs=in_specs, out_specs=out_specs, check_vma=False
    )
```

```python
import functools

import jax
import jax.numpy as jnp
from jax import lax
from jax.experimental import pallas as pl
from jax.experimental.pallas import tpu as pltpu
from jax.sharding import PartitionSpec as P

WINDOW = 1024
norm_epsilon = 1e-06
score_scale = 168.0 ** (-0.5)
rope_theta = 10000.0
MESH = pl.DeviceIdType.MESH
f32 = jnp.float32
bf16 = jnp.bfloat16


def dot(a, b, ca, cb):
    return lax.dot_general(a, b, (((ca,), (cb,)), ((), ())), preferred_element_type=f32)


def rope(n, cosines, sines, half):
    return n * cosines + pltpu.roll(n, half, 1) * sines


def rope_back(g, cosines, sines, half):
    return g * cosines + pltpu.roll(g * sines, half, 1)


def inverse_rms(u):
    return lax.rsqrt(jnp.mean(u * u, axis=-1, keepdims=True) + norm_epsilon)


def norm_rope_back(g, u, gain, cosines, sines, half):
    r = inverse_rms(u)
    w = rope_back(g, cosines, sines, half) * gain
    return r * (w - u * (r * r * jnp.mean(w * u, axis=-1, keepdims=True)))


def kernel(
    n_ctx, n_tp, reach, per_kv, kv_count, head, tile,
    tokens, rgrad, qw, kw, vw, ow, qgain, kgain, freq,
    out_ref, gout_ref,
    wqkv, wo, xg, gg, raw, cos_t, sin_t, q_s, do_s, dot_s, kv_own, halo, e_s, dp_s,
    l_s, ot_s, dqt_s, att, dkv, sum4, own_grad, gin, rin, zbuf, back, part, rs_in, stage,
    local_sem, ag_send, ag_recv, f_send, f_relay, f_recv, b_send, g_recv, r_recv,
    rs_send, rs_recv, out_sem,
):
    c = lax.axis_index("ctx")
    t = lax.axis_index("tp")
    s = lax.rem(c, reach)
    z = lax.div(c, reach)
    nz = n_ctx // reach
    local, width = xg.shape[1], xg.shape[2]
    rows = local * n_tp
    half = head // 2
    qc = kv_count * per_kv * head
    kc = kv_count * head
    qn = per_kv * rows

    def local_copy(i, src, dst):
        return pltpu.make_async_copy(src, dst, local_sem.at[i])

    loads = [
        local_copy(0, tokens, xg.at[0]),
        local_copy(1, kw, wqkv.at[:, qc : qc + kc]),
        local_copy(2, vw, wqkv.at[:, qc + kc : qc + 2 * kc]),
        local_copy(3, qw, wqkv.at[:, :qc]),
        local_copy(4, rgrad, gg.at[0]),
        local_copy(5, ow, wo),
    ]
    for load in loads:
        load.start()

    def to_ctx(src, dst, send, recv, target):
        return pltpu.make_async_remote_copy(
            src_ref=src, dst_ref=dst, send_sem=send, recv_sem=recv,
            device_id={"ctx": target}, device_id_type=MESH,
        )

    def to_tp(src, dst, send, recv, target):
        return pltpu.make_async_remote_copy(
            src_ref=src, dst_ref=dst, send_sem=send, recv_sem=recv,
            device_id={"tp": target}, device_id_type=MESH,
        )

    barrier = pltpu.get_barrier_semaphore()
    for j in range(1, n_tp):
        pl.semaphore_signal(
            barrier, inc=1, device_id={"tp": lax.rem(t + j, n_tp)}, device_id_type=MESH
        )
    for j in range(1, reach):
        mate = z * reach + lax.rem(s + j, reach)
        pl.semaphore_signal(barrier, inc=1, device_id={"ctx": mate}, device_id_type=MESH)

    @pl.when(z + 1 < nz)
    def _():
        pl.semaphore_signal(barrier, inc=1, device_id={"ctx": c + reach}, device_id_type=MESH)

    @pl.when(z > 0)
    def _():
        pl.semaphore_signal(barrier, inc=1, device_id={"ctx": c - reach}, device_id_type=MESH)

    up = 2 * reach - 1 - 2 * s
    down = 2 * s + 1
    upper = (z + 1 < nz) & (up < reach)
    lower = (z > 0) & (down < reach)

    @pl.when(upper)
    def _():
        pl.semaphore_signal(barrier, inc=1, device_id={"ctx": c + up}, device_id_type=MESH)

    @pl.when(lower)
    def _():
        pl.semaphore_signal(barrier, inc=1, device_id={"ctx": c - down}, device_id_type=MESH)

    one, none = jnp.int32(1), jnp.int32(0)
    greeted = (
        n_tp - 1 + reach - 1
        + jnp.where(z > 0, one, none)
        + jnp.where(z + 1 < nz, one, none)
        + jnp.where(upper, one, none)
        + jnp.where(lower, one, none)
    )
    def place(row):
        return lax.rem(t + lax.div(row, local), n_tp) * local + lax.rem(row, local)

    row = lax.broadcasted_iota(jnp.int32, (rows, head), 0)
    angles = (c * rows + place(row)).astype(f32) * freq[...]
    lane = lax.broadcasted_iota(jnp.int32, (rows, head), 1)
    cos_t[...] = jnp.cos(angles)
    sines = jnp.sin(angles)
    sin_t[...] = jnp.where(lane < half, -sines, sines)
    pl.semaphore_wait(barrier, greeted)

    gathers = []
    for w, (src, dst) in enumerate(((tokens, xg), (rgrad, gg))):
        for j in range(1, n_tp):
            copy = to_tp(src, dst.at[n_tp - j], ag_send.at[w, j - 1], ag_recv.at[w, j - 1],
                         lax.rem(t + j, n_tp))
            copy.start()
            gathers.append((w, copy))

    spans = (slice(0, local), slice(local, rows))

    def key_values(w, x):
        span = spans[w]
        raw[span, qc : qc + 2 * kc] = dot(x, wqkv[:, qc : qc + 2 * kc], 1, 0)
        for m in range(kv_count):
            u = raw[span, qc + m * head : qc + (m + 1) * head]
            n = u * inverse_rms(u) * kgain[...]
            kv_own[0, m, span] = rope(n, cos_t[span, :], sin_t[span, :], half).astype(bf16)
            v0 = qc + kc + m * head
            kv_own[1, m, span] = raw[span, v0 : v0 + head].astype(bf16)

    def ahead(w):
        return to_ctx(kv_own.at[:, :, spans[w]], halo.at[reach - 1, :, :, spans[w]],
                      f_send.at[reach - 1, w], f_recv.at[reach - 1, w], c + reach)

    def own_to(k, w):
        return to_ctx(kv_own.at[:, :, spans[w]], halo.at[k - 1, :, :, spans[w]],
                      f_send.at[k - 1, w], f_recv.at[k - 1, w], c + k)

    def relay_to(k, w):
        return to_ctx(halo.at[reach - 1, :, :, spans[w]],
                      halo.at[reach - k - 1, :, :, spans[w]], f_relay.at[k - 1, w],
                      f_recv.at[reach - k - 1, w], c - k)

    def halo_wait(d, w):
        own_span = kv_own.at[:, :, spans[w]]
        to_ctx(own_span, halo.at[d - 1, :, :, spans[w]], f_send.at[d - 1, w],
               f_recv.at[d - 1, w], c).wait_recv()

    def sends_own(k):
        return (s + k < reach) | (upper & (up == k))

    def relays(k):
        return (k <= s) & (2 * s - k != reach - 1)

    for w in range(2):
        if w == 0:
            for i in (0, 1, 2):
                loads[i].wait()
            key_values(w, xg[0])
        else:
            for which, copy in gathers:
                if which == 0:
                    copy.wait_recv()
            key_values(w, xg[1:].reshape(rows - local, width))

        @pl.when(z + 1 < nz)
        def _(w=w):
            ahead(w).start()

        for k in range(1, reach):
            @pl.when(sends_own(k))
            def _(k=k, w=w):
                own_to(k, w).start()

    loads[3].wait()
    raw[:, :qc] = dot(xg[...].reshape(rows, width), wqkv[:, :qc], 1, 0)
    for h in range(kv_count * per_kv):
        m, g = h // per_kv, h % per_kv
        u = raw[:, h * head : (h + 1) * head]
        n = u * inverse_rms(u) * qgain[...]
        q_s[m, g * rows : (g + 1) * rows] = rope(n, cos_t[...], sin_t[...], half).astype(bf16)
    loads[4].wait()
    loads[5].wait()
    for w, copy in gathers:
        if w == 1:
            copy.wait_recv()
    d_out = dot(gg[...].reshape(rows, width), wo[...], 1, 1).astype(bf16)
    for h in range(kv_count * per_kv):
        m, g = h // per_kv, h % per_kv
        piece = d_out[:, h * head : (h + 1) * head]
        do_s[m, g * rows : (g + 1) * rows] = piece
        dot_s[m, :, g * rows : (g + 1) * rows] = piece.astype(f32).T

    def kv(d, w, m):
        return kv_own[w, m] if d == 0 else halo[d - 1, w, m]

    def first_pass(d):
        for m in range(kv_count):
            key, value = kv(d, 0, m), kv(d, 1, m)
            e = jnp.exp(dot(key, q_s[m], 1, 1) * score_scale)
            if d == 0 or d == reach:
                key_row = place(lax.broadcasted_iota(jnp.int32, (rows, 1), 0))
                query_row = place(
                    lax.rem(lax.broadcasted_iota(jnp.int32, (1, qn), 1), jnp.int32(rows))
                )
                keep = query_row >= key_row if d == 0 else query_row < key_row
                e = jnp.where(keep, e, f32(0.0))
            total = jnp.sum(e, axis=0, keepdims=True)
            low = e.astype(bf16)
            e_s[d, m] = low
            mixed = dot(value, low, 0, 0)
            dp_s[d, m] = dot(value, do_s[m], 1, 1) * score_scale
            if d == 0:
                l_s[m] = total
                ot_s[m] = mixed
            else:
                l_s[m] += total
                ot_s[m] += mixed

    first_pass(0)

    @pl.when(z > 0)
    def _():
        for w in range(2):
            halo_wait(reach, w)
            for k in range(1, reach):
                @pl.when(relays(k))
                def _(k=k, w=w):
                    relay_to(k, w).start()
        first_pass(reach)

    for d in range(1, reach):
        @pl.when(c >= d)
        def _(d=d):
            halo_wait(d, 0)
            halo_wait(d, 1)
            first_pass(d)

    inv, delta = [], []
    for m in range(kv_count):
        inv.append(1.0 / l_s[m])
        o_t = (ot_s[m] * inv[m]).astype(bf16).astype(f32)
        delta.append(jnp.sum(o_t * dot_s[m], axis=0, keepdims=True) * score_scale)
        for g in range(per_kv):
            h = m * per_kv + g
            att[:, h * head : (h + 1) * head] = o_t[:, g * rows : (g + 1) * rows].T.astype(bf16)
        l_s[m] = inv[m]
        dqt_s[m] = jnp.zeros_like(dqt_s[m])

    def second_pass(d, m):
        p = e_s[d, m].astype(f32) * inv[m]
        ds = (p * (dp_s[d, m] - delta[m])).astype(bf16)
        dk = dot(ds, q_s[m], 1, 0)
        dv = dot(p.astype(bf16), do_s[m], 1, 0)
        dqt_s[m] += dot(kv(d, 0, m), ds, 0, 0)
        return dk, dv

    def grad_home(d, w):
        return to_ctx(dkv.at[d - 1, :, :, spans[w]], gin.at[d - 1, :, :, spans[w]],
                      b_send.at[d - 1, w], g_recv.at[d - 1, w], c - d)

    def grad_mate(d, w):
        k = reach - d
        return to_ctx(dkv.at[d - 1, :, :, spans[w]], rin.at[k - 1, :, :, spans[w]],
                      b_send.at[d - 1, w], r_recv.at[k - 1, w], c + k)

    def grad_back(w):
        return to_ctx(zbuf.at[:, :, spans[w]], gin.at[reach - 1, :, :, spans[w]],
                      b_send.at[reach - 1, w], g_recv.at[reach - 1, w], c - reach)

    for d in range(reach - 1, 0, -1):
        @pl.when(c >= d)
        def _(d=d):
            for m in range(kv_count):
                dk, dv = second_pass(d, m)
                dkv[d - 1, 0, m] = dk.astype(bf16)
                dkv[d - 1, 1, m] = dv.astype(bf16)

            for w in (1, 0):
                @pl.when((d <= s) | (d == down))
                def _(w=w):
                    grad_home(d, w).start()

                @pl.when((d > s) & (d != down))
                def _(w=w):
                    grad_mate(d, w).start()

    @pl.when(z > 0)
    def _():
        for m in range(kv_count):
            dk, dv = second_pass(reach, m)
            sum4[0, m] = dk
            sum4[1, m] = dv

    for m in range(kv_count):
        dk, dv = second_pass(0, m)
        own_grad[0, m] = dk
        own_grad[1, m] = dv

    def rs_copy(w, j):
        return to_tp(part.at[w, j], rs_in.at[w, j - 1], rs_send.at[w, j - 1],
                     rs_recv.at[w, j - 1], lax.rem(t + j, n_tp))

    def project(w, lhs, index, by_row):
        block = lhs[index * local : (index + 1) * local, :]

        def step(i, carry):
            cols = pl.ds(pl.multiple_of(i * tile, 128), tile)
            if by_row:
                part[w, index, :, cols] = dot(block, wo[:, cols], 1, 0).astype(bf16)
            else:
                part[w, index, :, cols] = dot(block, wqkv[cols, :], 1, 1).astype(bf16)
            return carry

        lax.fori_loop(0, width // tile, step, 0)

    for j in range(1, n_tp):
        project(0, att, j, True)
        rs_copy(0, j).start()

    @pl.when(z > 0)
    def _():
        for w in (1, 0):
            span = spans[w]
            for k in range(1, reach):
                @pl.when(relays(k))
                def _(k=k, w=w, span=span):
                    to_ctx(zbuf.at[:, :, span], rin.at[k - 1, :, :, span], b_send.at[k - 1, w],
                           r_recv.at[k - 1, w], c).wait_recv()
                    sum4[:, :, span] += rin[k - 1, :, :, span].astype(f32)
            zbuf[:, :, span] = sum4[:, :, span].astype(bf16)
            grad_back(w).start()

    for m in range(kv_count):
        for g in range(per_kv):
            h = m * per_kv + g
            grad = dqt_s[m, :, g * rows : (g + 1) * rows].T
            u = raw[:, h * head : (h + 1) * head]
            back[:, h * head : (h + 1) * head] = norm_rope_back(
                grad, u, qgain[...], cos_t[...], sin_t[...], half
            ).astype(bf16)

    project(0, att, 0, True)

    def finish(w, base, dst):
        total = part[w, 0].astype(f32)
        for j in range(1, n_tp):
            rs_copy(w, j).wait_recv()
            total += rs_in[w, j - 1].astype(f32)
        stage[w] = (base[0].astype(f32) + total).astype(bf16)
        copy = pltpu.make_async_copy(stage.at[w], dst, out_sem.at[w])
        copy.start()
        return copy

    written = [finish(0, xg, out_ref)]

    def gin_add(d, w):
        span = spans[w]
        to_ctx(zbuf.at[:, :, span], gin.at[d - 1, :, :, span], b_send.at[d - 1, w],
               g_recv.at[d - 1, w], c).wait_recv()
        own_grad[:, :, span] += gin[d - 1, :, :, span].astype(f32)

    for w in (1, 0):
        span = spans[w]
        for d in range(1, reach):
            @pl.when(sends_own(d))
            def _(d=d, w=w):
                gin_add(d, w)

        @pl.when(z + 1 < nz)
        def _(w=w):
            gin_add(reach, w)

        for m in range(kv_count):
            k0 = qc + m * head
            u = raw[span, k0 : k0 + head]
            back[span, k0 : k0 + head] = norm_rope_back(
                own_grad[0, m, span], u, kgain[...], cos_t[span, :], sin_t[span, :], half
            ).astype(bf16)
            back[span, k0 + kc : k0 + kc + head] = own_grad[1, m, span].astype(bf16)

        if w == 0:
            project(1, back, 0, False)
        else:
            for j in range(1, n_tp):
                project(1, back, j, False)
                rs_copy(1, j).start()
    written.append(finish(1, gg, gout_ref))

    for w, copy in gathers:
        copy.wait_send()

    for w in range(2):
        @pl.when(z + 1 < nz)
        def _(w=w):
            ahead(w).wait_send()

        for k in range(1, reach):
            @pl.when(sends_own(k))
            def _(k=k, w=w):
                own_to(k, w).wait_send()

            @pl.when((z > 0) & relays(k))
            def _(k=k, w=w):
                relay_to(k, w).wait_send()

            @pl.when(c >= k)
            def _(k=k, w=w):
                grad_home(k, w).wait_send()

        @pl.when(z > 0)
        def _(w=w):
            grad_back(w).wait_send()

    for w in range(2):
        for j in range(1, n_tp):
            rs_copy(w, j).wait_send()
    for copy in written:
        copy.wait()


def on_device(
    tokens, result_grad, query_weight, key_weight, value_weight, output_weight, query_gain, key_gain
):
    n_ctx = lax.axis_size("ctx")
    n_tp = lax.axis_size("tp")
    local, width = tokens.shape
    rows = local * n_tp
    head = query_gain.shape[0]
    kv_count = key_weight.shape[1] // head
    per_kv = query_weight.shape[1] // key_weight.shape[1]
    reach = WINDOW // rows
    qc = kv_count * per_kv * head
    kc = kv_count * head
    qn = per_kv * rows
    tile = max(k for k in range(128, 1025, 128) if width % k == 0)
    exponent = jnp.arange(head // 2, dtype=f32) * (2.0 / head)
    frequency = jnp.power(f32(rope_theta), -exponent)
    frequency = jnp.concatenate([frequency, frequency])[None, :]
    any_spec = pl.BlockSpec(memory_space=pl.ANY)
    vmem_spec = pl.BlockSpec(memory_space=pltpu.VMEM)
    block = (2, kv_count, rows, head)
    dma = pltpu.SemaphoreType.DMA
    out = jax.ShapeDtypeStruct((local, width), bf16)
    return pl.pallas_call(
        functools.partial(kernel, n_ctx, n_tp, reach, per_kv, kv_count, head, tile),
        out_shape=(out, out),
        in_specs=[any_spec] * 6 + [vmem_spec] * 3,
        out_specs=(any_spec, any_spec),
        scratch_shapes=[
            pltpu.VMEM((width, qc + 2 * kc), bf16),
            pltpu.VMEM((qc, width), bf16),
            pltpu.VMEM((n_tp, local, width), bf16),
            pltpu.VMEM((n_tp, local, width), bf16),
            pltpu.VMEM((rows, qc + 2 * kc), f32),
            pltpu.VMEM((rows, head), f32),
            pltpu.VMEM((rows, head), f32),
            pltpu.VMEM((kv_count, qn, head), bf16),
            pltpu.VMEM((kv_count, qn, head), bf16),
            pltpu.VMEM((kv_count, head, qn), f32),
            pltpu.VMEM(block, bf16),
            pltpu.VMEM((reach,) + block, bf16),
            pltpu.VMEM((reach + 1, kv_count, rows, qn), bf16),
            pltpu.VMEM((reach + 1, kv_count, rows, qn), f32),
            pltpu.VMEM((kv_count, 1, qn), f32),
            pltpu.VMEM((kv_count, head, qn), f32),
            pltpu.VMEM((kv_count, head, qn), f32),
            pltpu.VMEM((rows, qc), bf16),
            pltpu.VMEM((reach - 1,) + block, bf16),
            pltpu.VMEM(block, f32),
            pltpu.VMEM(block, f32),
            pltpu.VMEM((reach,) + block, bf16),
            pltpu.VMEM((reach - 1,) + block, bf16),
            pltpu.VMEM(block, bf16),
            pltpu.VMEM((rows, qc + 2 * kc), bf16),
            pltpu.VMEM((2, n_tp, local, width), bf16),
            pltpu.VMEM((2, n_tp - 1, local, width), bf16),
            pltpu.VMEM((2, local, width), bf16),
            dma((6,)),
            dma((2, n_tp - 1)),
            dma((2, n_tp - 1)),
            dma((reach, 2)),
            dma((reach - 1, 2)),
            dma((reach, 2)),
            dma((reach, 2)),
            dma((reach, 2)),
            dma((reach - 1, 2)),
            dma((2, n_tp - 1)),
            dma((2, n_tp - 1)),
            dma((2,)),
        ],
        compiler_params=pltpu.CompilerParams(
            collective_id=0, has_side_effects=True, vmem_limit_bytes=60 * 1024 * 1024
        ),
    )(
        tokens, result_grad, query_weight, key_weight, value_weight, output_weight,
        query_gain[None, :], key_gain[None, :], frequency,
    )


def solution(mesh):
    in_specs = (
        P(("ctx", "tp"), None),
        P(("ctx", "tp"), None),
        P(None, "tp"),
        P(None, "tp"),
        P(None, "tp"),
        P("tp", None),
        P(),
        P(),
    )
    out_specs = (P(("ctx", "tp"), None), P(("ctx", "tp"), None))
    return jax.shard_map(
        on_device, mesh=mesh, in_specs=in_specs, out_specs=out_specs, check_vma=False
    )
```

```python
import functools

import jax
import jax.numpy as jnp
import numpy as np
from jax import lax
from jax.experimental import pallas as pl
from jax.experimental.pallas import tpu as pltpu
from jax.sharding import PartitionSpec as P

WINDOW = 1024
norm_epsilon = 1e-06
score_scale = 168.0 ** (-0.5)
rope_theta = 10000.0
MESH = pl.DeviceIdType.MESH
f32 = jnp.float32
bf16 = jnp.bfloat16


def dot(a, b, ca, cb):
    return lax.dot_general(a, b, (((ca,), (cb,)), ((), ())), preferred_element_type=f32)


def rope(n, cosines, sines, half):
    return n * cosines + pltpu.roll(n, half, 1) * sines


def rope_back(g, cosines, sines, half):
    return g * cosines + pltpu.roll(g * sines, half, 1)


def inverse_rms(u):
    return lax.rsqrt(jnp.mean(u * u, axis=-1, keepdims=True) + norm_epsilon)


def norm_rope_back(g, u, gain, cosines, sines, half):
    r = inverse_rms(u)
    w = rope_back(g, cosines, sines, half) * gain
    return r * (w - u * (r * r * jnp.mean(w * u, axis=-1, keepdims=True)))


def kernel(
    n_ctx, n_tp, reach, per_kv, kv_count, head, tile,
    tokens, rgrad, qw, kw, vw, ow, qgain, kgain, freq,
    out_ref, gout_ref,
    wqkv, wo, xg, gg, raw, cos_t, sin_t, q_s, do_s, dot_s, kv_own, halo, e_s, dp_s,
    l_s, ot_s, dqt_s, att, dkv, sum4, own_grad, gin, rin, zbuf, back, part, rs_in, stage,
    local_sem, ag_send, ag_recv, f_send, f_relay, f_recv, b_send, g_recv, r_recv,
    rs_send, rs_recv, out_sem,
):
    c = lax.axis_index("ctx")
    t = lax.axis_index("tp")
    s = lax.rem(c, reach)
    z = lax.div(c, reach)
    nz = n_ctx // reach
    local, width = xg.shape[1], xg.shape[2]
    rows = local * n_tp
    half = head // 2
    qc = kv_count * per_kv * head
    kc = kv_count * head
    qn = per_kv * rows

    def local_copy(i, src, dst):
        return pltpu.make_async_copy(src, dst, local_sem.at[i])

    loads = [
        local_copy(0, tokens, xg.at[0]),
        local_copy(1, kw, wqkv.at[:, qc : qc + kc]),
        local_copy(2, vw, wqkv.at[:, qc + kc : qc + 2 * kc]),
        local_copy(3, qw, wqkv.at[:, :qc]),
        local_copy(4, rgrad, gg.at[0]),
        local_copy(5, ow, wo),
    ]
    for load in loads:
        load.start()

    def to_ctx(src, dst, send, recv, target):
        return pltpu.make_async_remote_copy(
            src_ref=src, dst_ref=dst, send_sem=send, recv_sem=recv,
            device_id={"ctx": target}, device_id_type=MESH,
        )

    def to_tp(src, dst, send, recv, target):
        return pltpu.make_async_remote_copy(
            src_ref=src, dst_ref=dst, send_sem=send, recv_sem=recv,
            device_id={"tp": target}, device_id_type=MESH,
        )

    barrier = pltpu.get_barrier_semaphore()
    for j in range(1, n_tp):
        pl.semaphore_signal(
            barrier, inc=1, device_id={"tp": lax.rem(t + j, n_tp)}, device_id_type=MESH
        )
    for j in range(1, reach):
        mate = z * reach + lax.rem(s + j, reach)
        pl.semaphore_signal(barrier, inc=1, device_id={"ctx": mate}, device_id_type=MESH)

    @pl.when(z + 1 < nz)
    def _():
        pl.semaphore_signal(barrier, inc=1, device_id={"ctx": c + reach}, device_id_type=MESH)

    @pl.when(z > 0)
    def _():
        pl.semaphore_signal(barrier, inc=1, device_id={"ctx": c - reach}, device_id_type=MESH)

    up = 2 * reach - 1 - 2 * s
    down = 2 * s + 1
    upper = (z + 1 < nz) & (up < reach)
    lower = (z > 0) & (down < reach)

    @pl.when(upper)
    def _():
        pl.semaphore_signal(barrier, inc=1, device_id={"ctx": c + up}, device_id_type=MESH)

    @pl.when(lower)
    def _():
        pl.semaphore_signal(barrier, inc=1, device_id={"ctx": c - down}, device_id_type=MESH)

    one, none = jnp.int32(1), jnp.int32(0)
    greeted = (
        n_tp - 1 + reach - 1
        + jnp.where(z > 0, one, none)
        + jnp.where(z + 1 < nz, one, none)
        + jnp.where(upper, one, none)
        + jnp.where(lower, one, none)
    )
    def place(row):
        return lax.rem(t + lax.div(row, local), n_tp) * local + lax.rem(row, local)

    row = lax.broadcasted_iota(jnp.int32, (rows, head), 0)
    angles = (c * rows + place(row)).astype(f32) * freq[...]
    lane = lax.broadcasted_iota(jnp.int32, (rows, head), 1)
    cos_t[...] = jnp.cos(angles)
    sines = jnp.sin(angles)
    sin_t[...] = jnp.where(lane < half, -sines, sines)
    pl.semaphore_wait(barrier, greeted)

    gathers = []
    for w, (src, dst) in enumerate(((tokens, xg), (rgrad, gg))):
        for j in range(1, n_tp):
            copy = to_tp(src, dst.at[n_tp - j], ag_send.at[w, j - 1], ag_recv.at[w, j - 1],
                         lax.rem(t + j, n_tp))
            copy.start()
            gathers.append((w, copy))

    spans = (slice(0, local), slice(local, rows))

    def key_values(w, x):
        span = spans[w]
        raw[span, qc : qc + 2 * kc] = dot(x, wqkv[:, qc : qc + 2 * kc], 1, 0)
        for m in range(kv_count):
            u = raw[span, qc + m * head : qc + (m + 1) * head]
            n = u * inverse_rms(u) * kgain[...]
            kv_own[0, m, span] = rope(n, cos_t[span, :], sin_t[span, :], half).astype(bf16)
            v0 = qc + kc + m * head
            kv_own[1, m, span] = raw[span, v0 : v0 + head].astype(bf16)

    def ahead(w):
        return to_ctx(kv_own.at[:, :, spans[w]], halo.at[reach - 1, :, :, spans[w]],
                      f_send.at[reach - 1, w], f_recv.at[reach - 1, w], c + reach)

    def own_to(k, w):
        return to_ctx(kv_own.at[:, :, spans[w]], halo.at[k - 1, :, :, spans[w]],
                      f_send.at[k - 1, w], f_recv.at[k - 1, w], c + k)

    def relay_to(k, w):
        return to_ctx(halo.at[reach - 1, :, :, spans[w]],
                      halo.at[reach - k - 1, :, :, spans[w]], f_relay.at[k - 1, w],
                      f_recv.at[reach - k - 1, w], c - k)

    def halo_wait(d, w):
        own_span = kv_own.at[:, :, spans[w]]
        to_ctx(own_span, halo.at[d - 1, :, :, spans[w]], f_send.at[d - 1, w],
               f_recv.at[d - 1, w], c).wait_recv()

    def sends_own(k):
        return (s + k < reach) | (upper & (up == k))

    def relays(k):
        return (k <= s) & (2 * s - k != reach - 1)

    for w in range(2):
        if w == 0:
            for i in (0, 1, 2):
                loads[i].wait()
            key_values(w, xg[0])
        else:
            for which, copy in gathers:
                if which == 0:
                    copy.wait_recv()
            key_values(w, xg[1:].reshape(rows - local, width))

        for k in range(1, reach):
            @pl.when(upper & (up == k))
            def _(k=k, w=w):
                own_to(k, w).start()

        @pl.when(z + 1 < nz)
        def _(w=w):
            ahead(w).start()

        for k in range(reach - 1, 0, -1):
            @pl.when(s + k < reach)
            def _(k=k, w=w):
                own_to(k, w).start()

    loads[3].wait()
    raw[:, :qc] = dot(xg[...].reshape(rows, width), wqkv[:, :qc], 1, 0)
    for h in range(kv_count * per_kv):
        m, g = h // per_kv, h % per_kv
        u = raw[:, h * head : (h + 1) * head]
        n = u * inverse_rms(u) * qgain[...]
        q_s[m, g * rows : (g + 1) * rows] = rope(n, cos_t[...], sin_t[...], half).astype(bf16)
    loads[4].wait()
    loads[5].wait()
    for w, copy in gathers:
        if w == 1:
            copy.wait_recv()
    d_out = dot(gg[...].reshape(rows, width), wo[...], 1, 1).astype(bf16)
    for h in range(kv_count * per_kv):
        m, g = h // per_kv, h % per_kv
        piece = d_out[:, h * head : (h + 1) * head]
        do_s[m, g * rows : (g + 1) * rows] = piece
        dot_s[m, :, g * rows : (g + 1) * rows] = piece.astype(f32).T

    def kv(d, w, m):
        return kv_own[w, m] if d == 0 else halo[d - 1, w, m]

    def first_pass(d):
        for m in range(kv_count):
            key, value = kv(d, 0, m), kv(d, 1, m)
            e = jnp.exp(dot(key, q_s[m], 1, 1) * score_scale)
            if d == 0 or d == reach:
                key_row = place(lax.broadcasted_iota(jnp.int32, (rows, 1), 0))
                query_row = place(
                    lax.rem(lax.broadcasted_iota(jnp.int32, (1, qn), 1), jnp.int32(rows))
                )
                keep = query_row >= key_row if d == 0 else query_row < key_row
                e = jnp.where(keep, e, f32(0.0))
            total = jnp.sum(e, axis=0, keepdims=True)
            low = e.astype(bf16)
            e_s[d, m] = low
            mixed = dot(value, low, 0, 0)
            dp_s[d, m] = dot(value, do_s[m], 1, 1) * score_scale
            if d == 0:
                l_s[m] = total
                ot_s[m] = mixed
            else:
                l_s[m] += total
                ot_s[m] += mixed

    first_pass(0)

    @pl.when(z > 0)
    def _():
        for w in range(2):
            halo_wait(reach, w)
            for k in range(1, reach):
                @pl.when(relays(k))
                def _(k=k, w=w):
                    relay_to(k, w).start()
        first_pass(reach)

    for d in range(1, reach):
        @pl.when(c >= d)
        def _(d=d):
            halo_wait(d, 0)
            halo_wait(d, 1)
            first_pass(d)

    inv, delta = [], []
    for m in range(kv_count):
        inv.append(1.0 / l_s[m])
        o_t = (ot_s[m] * inv[m]).astype(bf16).astype(f32)
        delta.append(jnp.sum(o_t * dot_s[m], axis=0, keepdims=True) * score_scale)
        for g in range(per_kv):
            h = m * per_kv + g
            att[:, h * head : (h + 1) * head] = o_t[:, g * rows : (g + 1) * rows].T.astype(bf16)
        l_s[m] = inv[m]
        dqt_s[m] = jnp.zeros_like(dqt_s[m])

    def second_pass(d, m):
        p = e_s[d, m].astype(f32) * inv[m]
        ds = (p * (dp_s[d, m] - delta[m])).astype(bf16)
        dk = dot(ds, q_s[m], 1, 0)
        dv = dot(p.astype(bf16), do_s[m], 1, 0)
        dqt_s[m] += dot(kv(d, 0, m), ds, 0, 0)
        return dk, dv

    def grad_home(d, w):
        return to_ctx(dkv.at[d - 1, :, :, spans[w]], gin.at[d - 1, :, :, spans[w]],
                      b_send.at[d - 1, w], g_recv.at[d - 1, w], c - d)

    def grad_mate(d, w):
        k = reach - d
        return to_ctx(dkv.at[d - 1, :, :, spans[w]], rin.at[k - 1, :, :, spans[w]],
                      b_send.at[d - 1, w], r_recv.at[k - 1, w], c + k)

    def grad_back(w):
        return to_ctx(zbuf.at[:, :, spans[w]], gin.at[reach - 1, :, :, spans[w]],
                      b_send.at[reach - 1, w], g_recv.at[reach - 1, w], c - reach)

    for d in range(reach - 1, 0, -1):
        @pl.when(c >= d)
        def _(d=d):
            for m in range(kv_count):
                dk, dv = second_pass(d, m)
                dkv[d - 1, 0, m] = dk.astype(bf16)
                dkv[d - 1, 1, m] = dv.astype(bf16)

            for w in (1, 0):
                @pl.when((d <= s) | (d == down))
                def _(w=w):
                    grad_home(d, w).start()

                @pl.when((d > s) & (d != down))
                def _(w=w):
                    grad_mate(d, w).start()

    @pl.when(z > 0)
    def _():
        for m in range(kv_count):
            dk, dv = second_pass(reach, m)
            sum4[0, m] = dk
            sum4[1, m] = dv

    for m in range(kv_count):
        dk, dv = second_pass(0, m)
        own_grad[0, m] = dk
        own_grad[1, m] = dv

    def rs_copy(w, j):
        return to_tp(part.at[w, j], rs_in.at[w, j - 1], rs_send.at[w, j - 1],
                     rs_recv.at[w, j - 1], lax.rem(t + j, n_tp))

    def project(w, lhs, index, by_row):
        block = lhs[index * local : (index + 1) * local, :]

        def step(i, carry):
            cols = pl.ds(pl.multiple_of(i * tile, 128), tile)
            if by_row:
                part[w, index, :, cols] = dot(block, wo[:, cols], 1, 0).astype(bf16)
            else:
                part[w, index, :, cols] = dot(block, wqkv[cols, :], 1, 1).astype(bf16)
            return carry

        lax.fori_loop(0, width // tile, step, 0)

    for j in range(1, n_tp):
        project(0, att, j, True)
        rs_copy(0, j).start()

    @pl.when(z > 0)
    def _():
        for w in (1, 0):
            span = spans[w]
            for k in range(1, reach):
                @pl.when(relays(k))
                def _(k=k, w=w, span=span):
                    to_ctx(zbuf.at[:, :, span], rin.at[k - 1, :, :, span], b_send.at[k - 1, w],
                           r_recv.at[k - 1, w], c).wait_recv()
                    sum4[:, :, span] += rin[k - 1, :, :, span].astype(f32)
            zbuf[:, :, span] = sum4[:, :, span].astype(bf16)
            grad_back(w).start()

    for m in range(kv_count):
        for g in range(per_kv):
            h = m * per_kv + g
            grad = dqt_s[m, :, g * rows : (g + 1) * rows].T
            u = raw[:, h * head : (h + 1) * head]
            back[:, h * head : (h + 1) * head] = norm_rope_back(
                grad, u, qgain[...], cos_t[...], sin_t[...], half
            ).astype(bf16)

    project(0, att, 0, True)

    def finish(w, base, dst):
        total = part[w, 0].astype(f32)
        for j in range(1, n_tp):
            rs_copy(w, j).wait_recv()
            total += rs_in[w, j - 1].astype(f32)
        stage[w] = (base[0].astype(f32) + total).astype(bf16)
        copy = pltpu.make_async_copy(stage.at[w], dst, out_sem.at[w])
        copy.start()
        return copy

    written = [finish(0, xg, out_ref)]

    def gin_add(d, w):
        span = spans[w]
        to_ctx(zbuf.at[:, :, span], gin.at[d - 1, :, :, span], b_send.at[d - 1, w],
               g_recv.at[d - 1, w], c).wait_recv()
        own_grad[:, :, span] += gin[d - 1, :, :, span].astype(f32)

    for w in (1, 0):
        span = spans[w]
        for d in range(1, reach):
            @pl.when(sends_own(d))
            def _(d=d, w=w):
                gin_add(d, w)

        @pl.when(z + 1 < nz)
        def _(w=w):
            gin_add(reach, w)

        for m in range(kv_count):
            k0 = qc + m * head
            u = raw[span, k0 : k0 + head]
            back[span, k0 : k0 + head] = norm_rope_back(
                own_grad[0, m, span], u, kgain[...], cos_t[span, :], sin_t[span, :], half
            ).astype(bf16)
            back[span, k0 + kc : k0 + kc + head] = own_grad[1, m, span].astype(bf16)

        if w == 0:
            project(1, back, 0, False)
        else:
            for j in range(1, n_tp):
                project(1, back, j, False)
                rs_copy(1, j).start()
    written.append(finish(1, gg, gout_ref))

    for w, copy in gathers:
        copy.wait_send()

    for w in range(2):
        @pl.when(z + 1 < nz)
        def _(w=w):
            ahead(w).wait_send()

        for k in range(1, reach):
            @pl.when(sends_own(k))
            def _(k=k, w=w):
                own_to(k, w).wait_send()

            @pl.when((z > 0) & relays(k))
            def _(k=k, w=w):
                relay_to(k, w).wait_send()

            @pl.when(c >= k)
            def _(k=k, w=w):
                grad_home(k, w).wait_send()

        @pl.when(z > 0)
        def _(w=w):
            grad_back(w).wait_send()

    for w in range(2):
        for j in range(1, n_tp):
            rs_copy(w, j).wait_send()
    for copy in written:
        copy.wait()


def on_device(
    tokens, result_grad, query_weight, key_weight, value_weight, output_weight, query_gain, key_gain
):
    n_ctx = lax.axis_size("ctx")
    n_tp = lax.axis_size("tp")
    local, width = tokens.shape
    rows = local * n_tp
    head = query_gain.shape[0]
    kv_count = key_weight.shape[1] // head
    per_kv = query_weight.shape[1] // key_weight.shape[1]
    reach = WINDOW // rows
    qc = kv_count * per_kv * head
    kc = kv_count * head
    qn = per_kv * rows
    tile = max(k for k in range(128, 1025, 128) if width % k == 0)
    exponent = np.arange(head // 2, dtype=np.float32) * np.float32(2.0 / head)
    frequency = np.power(np.float32(rope_theta), -exponent)
    frequency = jnp.asarray(np.concatenate([frequency, frequency])[None, :])
    any_spec = pl.BlockSpec(memory_space=pl.ANY)
    vmem_spec = pl.BlockSpec(memory_space=pltpu.VMEM)
    block = (2, kv_count, rows, head)
    dma = pltpu.SemaphoreType.DMA
    out = jax.ShapeDtypeStruct((local, width), bf16)
    return pl.pallas_call(
        functools.partial(kernel, n_ctx, n_tp, reach, per_kv, kv_count, head, tile),
        out_shape=(out, out),
        in_specs=[any_spec] * 6 + [vmem_spec] * 3,
        out_specs=(any_spec, any_spec),
        scratch_shapes=[
            pltpu.VMEM((width, qc + 2 * kc), bf16),
            pltpu.VMEM((qc, width), bf16),
            pltpu.VMEM((n_tp, local, width), bf16),
            pltpu.VMEM((n_tp, local, width), bf16),
            pltpu.VMEM((rows, qc + 2 * kc), f32),
            pltpu.VMEM((rows, head), f32),
            pltpu.VMEM((rows, head), f32),
            pltpu.VMEM((kv_count, qn, head), bf16),
            pltpu.VMEM((kv_count, qn, head), bf16),
            pltpu.VMEM((kv_count, head, qn), f32),
            pltpu.VMEM(block, bf16),
            pltpu.VMEM((reach,) + block, bf16),
            pltpu.VMEM((reach + 1, kv_count, rows, qn), bf16),
            pltpu.VMEM((reach + 1, kv_count, rows, qn), f32),
            pltpu.VMEM((kv_count, 1, qn), f32),
            pltpu.VMEM((kv_count, head, qn), f32),
            pltpu.VMEM((kv_count, head, qn), f32),
            pltpu.VMEM((rows, qc), bf16),
            pltpu.VMEM((reach - 1,) + block, bf16),
            pltpu.VMEM(block, f32),
            pltpu.VMEM(block, f32),
            pltpu.VMEM((reach,) + block, bf16),
            pltpu.VMEM((reach - 1,) + block, bf16),
            pltpu.VMEM(block, bf16),
            pltpu.VMEM((rows, qc + 2 * kc), bf16),
            pltpu.VMEM((2, n_tp, local, width), bf16),
            pltpu.VMEM((2, n_tp - 1, local, width), bf16),
            pltpu.VMEM((2, local, width), bf16),
            dma((6,)),
            dma((2, n_tp - 1)),
            dma((2, n_tp - 1)),
            dma((reach, 2)),
            dma((reach - 1, 2)),
            dma((reach, 2)),
            dma((reach, 2)),
            dma((reach, 2)),
            dma((reach - 1, 2)),
            dma((2, n_tp - 1)),
            dma((2, n_tp - 1)),
            dma((2,)),
        ],
        compiler_params=pltpu.CompilerParams(
            collective_id=0, has_side_effects=True, vmem_limit_bytes=60 * 1024 * 1024
        ),
    )(
        tokens, result_grad, query_weight, key_weight, value_weight, output_weight,
        query_gain[None, :], key_gain[None, :], frequency,
    )


def solution(mesh):
    in_specs = (
        P(("ctx", "tp"), None),
        P(("ctx", "tp"), None),
        P(None, "tp"),
        P(None, "tp"),
        P(None, "tp"),
        P("tp", None),
        P(),
        P(),
    )
    out_specs = (P(("ctx", "tp"), None), P(("ctx", "tp"), None))
    return jax.shard_map(
        on_device, mesh=mesh, in_specs=in_specs, out_specs=out_specs, check_vma=False
    )
```
